32 devices in a mesh: shot: 8 (over z, y), off: 4 (over x, core).
Axes of the slice: x: 2, y: 2, z: 4, core: 2. Of those that a mesh axis runs over, the one named last changes fastest.
Arguments:
- traces: bfloat16 [32, 768, 2048], P('shot', 'off'), may hold values from -60 to 60
- offset_bin: int32 [32, 768], P('shot', 'off'), may hold values from 0 to 31, as said below
- rec_id: int32 [32, 768], P('shot', 'off'), may hold values from 0 to 2047, as said below
- cmp_id: int32 [32, 768], P('shot', 'off'), may hold values from 0 to 4095, as said below
- rec_owner: int32 [2048], replicated, may hold values from 0 to 7, as said below
- rec_slot: int32 [2048], replicated, may hold values from 0 to 255
- cmp_owner: int32 [4096], replicated, may hold values from 0 to 7, as said below
- cmp_slot: int32 [4096], replicated, may hold values from 0 to 511
Outputs:
- source_term: float32 [32, 640], P('shot')
- offset_term: float32 [32, 640], P('off')
- receiver_term: float32 [2048, 640], P(('shot', 'off'))
- midpoint_term: float32 [4096, 640], P(('shot', 'off'))
The draws below stay inside these ranges and needn't reach their ends.
Inputs may be any that keep to these rules, and one draw needn't show every extreme that they name: `offset_bin`: a trace at position j of its shot has a bin of (j // 192) * 8 to (j // 192 + 1) * 8 - 1. rec_owner[r] * 256 + rec_slot[r] takes every value below 2048 exactly once. cmp_owner[c] * 512 + cmp_slot[c] takes every value below 4096 exactly once. `rec_id`: of the traces of one device's block (4 shots by 192 traces) at most 192 have receivers of any one owner; for every offset group some owner gets exactly 192 from every block of that group. `cmp_id`: of the traces of one device's block at most 192 have midpoints of any one owner; for every offset group some owner gets exactly 192 from every block of that group.
All inputs are finite; a program needn't handle non-finite values.
Results may differ from the reference program's by a relative error of at most 0.0035.
Values may be sent and summed in bfloat16 or wider, within the bound.
A program may use at most 64 MiB of HBM per device.

```python
import math
import jax
import jax.numpy as jnp
from jax import lax

NT = 2048
NF = 640
SHOT_DEV = 4
TR_OFF = 192
OFFB_DEV = 8
REC_DEV = 256
CMP_DEV = 512
SWEEPS = 2
SHOTS = 32
TR_SHOT = 768
NOFF = 32
NREC = 2048
NCMP = 4096
N_SHOT = 8
N_OFF = 4


def owner_tables(seed_key, count_dev):
    total_n = count_dev * N_SHOT
    shuffle = jax.random.permutation(seed_key, total_n).astype(jnp.int32)
    position = jnp.zeros((total_n,), jnp.int32).at[shuffle].set(jnp.arange(total_n, dtype=jnp.int32))
    return (position // count_dev, position % count_dev, shuffle)


def block_layout(values):
    shaped = values.reshape(N_SHOT, N_OFF, SHOT_DEV, TR_OFF)
    return jnp.transpose(shaped, (0, 2, 1, 3)).reshape(SHOTS, TR_SHOT)


def trace_ids(seed_key, count_dev):
    owners, places, shuffle = owner_tables(jax.random.fold_in(seed_key, 1), count_dev)
    per_dev = SHOT_DEV * TR_OFF
    capacity = 2 * per_dev // N_SHOT
    hottest = jax.random.randint(jax.random.fold_in(seed_key, 2), (1, N_OFF, 1), 0, N_SHOT)
    starting = jax.random.randint(jax.random.fold_in(seed_key, 3), (N_SHOT, N_OFF, 1), 0, N_SHOT - 1)
    position = jnp.arange(per_dev, dtype=jnp.int32)[None, None, :]
    cycled = (position - capacity + starting) % (N_SHOT - 1)
    others = cycled + (cycled >= hottest).astype(jnp.int32)
    owner_of = jnp.where(position < capacity, hottest, others)
    scores = jax.random.randint(jax.random.fold_in(seed_key, 4), (N_SHOT, N_OFF, per_dev), 0, 65536) * per_dev + position
    arrange = jnp.argsort(scores, axis=2, stable=True)
    owner_of = jnp.take_along_axis(owner_of, arrange, axis=2)
    slot_of = jax.random.randint(jax.random.fold_in(seed_key, 5), (N_SHOT, N_OFF, per_dev), 0, count_dev)
    identity = shuffle[owner_of * count_dev + slot_of]
    return (block_layout(identity), owners, places)


def bin_draw(seed_key):
    groups = jnp.arange(N_OFF, dtype=jnp.int32)[None, :, None]
    inside = jax.random.randint(seed_key, (N_SHOT, N_OFF, SHOT_DEV * TR_OFF), 0, OFFB_DEV)
    return block_layout(inside + groups * OFFB_DEV)


def draw_offset_bin(key, part):
    return bin_draw(jax.random.fold_in(key, 303))


def draw_rec_id(key, part):
    return trace_ids(jax.random.fold_in(key, 101), REC_DEV)[0]


def draw_rec_owner(key, part):
    return trace_ids(jax.random.fold_in(key, 101), REC_DEV)[1]


def draw_rec_slot(key, part):
    return trace_ids(jax.random.fold_in(key, 101), REC_DEV)[2]


def draw_cmp_id(key, part):
    return trace_ids(jax.random.fold_in(key, 202), CMP_DEV)[0]


def draw_cmp_owner(key, part):
    return trace_ids(jax.random.fold_in(key, 202), CMP_DEV)[1]


def draw_cmp_slot(key, part):
    return trace_ids(jax.random.fold_in(key, 202), CMP_DEV)[2]


def draw_traces(key, part):
    bins = bin_draw(jax.random.fold_in(key, 303))
    receivers = trace_ids(jax.random.fold_in(key, 101), REC_DEV)[0]
    midpoints = trace_ids(jax.random.fold_in(key, 202), CMP_DEV)[0]
    rec_gain = jax.random.uniform(jax.random.fold_in(key, 405), (NREC,), jnp.float32, -0.5, 0.5)
    cmp_gain = jax.random.uniform(jax.random.fold_in(key, 406), (NCMP,), jnp.float32, -0.4, 0.4)
    off_level = -1.0 * jnp.arange(NOFF, dtype=jnp.float32) / NOFF + jax.random.uniform(jax.random.fold_in(key, 407), (NOFF,), jnp.float32, -0.2, 0.2)
    shot_pos = jnp.arange(SHOTS, dtype=jnp.float32) / SHOTS
    jitter = jax.random.uniform(jax.random.fold_in(key, 408), (SHOTS,), jnp.float32, -0.3, 0.3)
    shot_level = 0.8 * shot_pos + jitter
    noise = jnp.clip(jax.random.normal(jax.random.fold_in(key, 409), (SHOTS, TR_SHOT, NT), jnp.float32), -6.0, 6.0)
    levels = shot_level[:, None] + off_level[bins] + rec_gain[receivers] + cmp_gain[midpoints]
    return jnp.clip(noise * jnp.exp(levels)[:, :, None], -60.0, 60.0).astype(jnp.bfloat16)


def setup_inputs(seed: int = 0) -> dict:
    keys = jax.random.split(jax.random.key(seed), 9)
    return {
        "traces": draw_traces(jax.random.fold_in(keys[8], 71), 0),
        "offset_bin": draw_offset_bin(jax.random.fold_in(keys[8], 71), 0),
        "rec_id": draw_rec_id(jax.random.fold_in(keys[8], 71), 0),
        "cmp_id": draw_cmp_id(jax.random.fold_in(keys[8], 71), 0),
        "rec_owner": draw_rec_owner(jax.random.fold_in(keys[8], 71), 0),
        "rec_slot": draw_rec_slot(jax.random.fold_in(keys[8], 71), 0),
        "cmp_owner": draw_cmp_owner(jax.random.fold_in(keys[8], 71), 0),
        "cmp_slot": draw_cmp_slot(jax.random.fold_in(keys[8], 71), 0),
    }


OMEGA = 0.35
FLOOR = 0.05

def spectral_table(samples, freqs):
    sample_idx = jnp.arange(samples, dtype=jnp.int32)
    freq_idx = jnp.arange(freqs, dtype=jnp.int32)
    phases = sample_idx[:, None] * freq_idx[None, :] % samples
    angles = phases.astype(jnp.float32) * (2.0 * math.pi / samples)
    tapers = 0.5 - 0.5 * jnp.cos((sample_idx.astype(jnp.float32) + 0.5) * (2.0 * math.pi / samples))
    weights = (tapers * math.sqrt(8.0 / (3.0 * samples)))[:, None]
    return jnp.concatenate([weights * jnp.cos(angles), -weights * jnp.sin(angles)], axis=1).astype(jnp.bfloat16)

def log_spectrum(shot_block, table, freqs):
    products = jnp.dot(shot_block, table, preferred_element_type=jnp.float32)
    real_part = products[:, :freqs]
    imag_part = products[:, freqs:]
    return jnp.log(real_part * real_part + imag_part * imag_part + FLOOR)

def reference(traces, offset_bin, rec_id, cmp_id, rec_owner, rec_slot, cmp_owner, cmp_slot):
    shots, tr_shot, samples = traces.shape
    table = spectral_table(samples, NF)
    logs = lax.map(lambda shot_block: log_spectrum(shot_block, table, NF), traces)
    bins = offset_bin.reshape(-1)
    receivers = rec_id.reshape(-1)
    midpoints = cmp_id.reshape(-1)
    unit = jnp.ones(bins.shape, jnp.float32)
    bin_count = jax.ops.segment_sum(unit, bins, NOFF)
    rec_count = jax.ops.segment_sum(unit, receivers, NREC)
    cmp_count = jax.ops.segment_sum(unit, midpoints, NCMP)
    source_term = jnp.zeros((shots, NF), jnp.float32)
    offset_term = jnp.zeros((NOFF, NF), jnp.float32)
    rec_term = jnp.zeros((NREC, NF), jnp.float32)
    cmp_term = jnp.zeros((NCMP, NF), jnp.float32)
    for sweep_no in range(SWEEPS):
        rec_trace = lax.optimization_barrier(rec_term.astype(jnp.bfloat16)).astype(jnp.float32)[receivers]
        cmp_trace = lax.optimization_barrier(cmp_term.astype(jnp.bfloat16)).astype(jnp.float32)[midpoints]
        per_shot = (logs - source_term[:, None, :]).reshape(shots * tr_shot, NF)
        residual = per_shot - offset_term[bins] - rec_trace - cmp_trace
        rounded = lax.optimization_barrier(residual.astype(jnp.bfloat16)).astype(jnp.float32)
        shot_sum = lax.optimization_barrier(jnp.sum(residual.reshape(shots, tr_shot, NF), axis=1))
        bin_sum = jax.ops.segment_sum(residual, bins, NOFF)
        rec_sum = jax.ops.segment_sum(rounded, receivers, NREC)
        cmp_sum = jax.ops.segment_sum(rounded, midpoints, NCMP)
        source_term = source_term + OMEGA * shot_sum / (tr_shot + 1.0)
        offset_term = offset_term + OMEGA * bin_sum / (bin_count[:, None] + 1.0)
        rec_term = rec_term + OMEGA * rec_sum / (rec_count[:, None] + 1.0)
        cmp_term = cmp_term + OMEGA * cmp_sum / (cmp_count[:, None] + 1.0)
    receiver_term = jnp.zeros_like(rec_term).at[rec_owner * REC_DEV + rec_slot].set(rec_term)
    midpoint_term = jnp.zeros_like(cmp_term).at[cmp_owner * CMP_DEV + cmp_slot].set(cmp_term)
    return (source_term, offset_term, receiver_term, midpoint_term)
```

```python
import math

import jax
import jax.numpy as jnp
from jax import lax
from jax.experimental import pallas as pl
from jax.experimental.pallas import tpu as pltpu
from jax.sharding import PartitionSpec as P

NF = 640
OFFB_DEV = 8
SWEEPS = 2
LANES = 128
WIDE = 256

OMEGA = 0.35
FLOOR = 0.05
VMEM_BYTES = 60 * 1024 * 1024


def up(value, unit):
    return -(-value // unit) * unit


def dot_nt(a, b):
    return lax.dot_general(a, b, (((1,), (1,)), ((), ())), preferred_element_type=jnp.float32)


def dot_nn(a, b):
    return lax.dot_general(a, b, (((1,), (0,)), ((), ())), preferred_element_type=jnp.float32)


def base_angles(samples, n_dev, held, padded):
    row = jnp.arange(n_dev * padded, dtype=jnp.int32)
    freq = ((row // padded) * held + row % padded)[:, None]
    coarse = jnp.arange(samples // LANES, dtype=jnp.int32)[None, :] * LANES
    fine = jnp.arange(LANES, dtype=jnp.int32)[None, :]
    step = 2.0 * math.pi / samples
    coarse_angle = (freq * coarse % samples).astype(jnp.float32) * step
    fine_angle = (freq * fine % samples).astype(jnp.float32) * step
    sample_idx = jnp.arange(samples, dtype=jnp.float32)[None, :]
    tapers = 0.5 - 0.5 * jnp.cos((sample_idx + 0.5) * step)
    weights = tapers * math.sqrt(8.0 / (3.0 * samples))
    return (
        jnp.cos(coarse_angle),
        jnp.sin(coarse_angle),
        jnp.cos(fine_angle),
        jnp.sin(fine_angle),
        weights,
    )


def logs_kernel(traces_ref, ca_ref, sa_ref, cb_ref, sb_ref, w_ref, out_ref, table):
    rows = ca_ref.shape[0]
    cb = cb_ref[...]
    sb = sb_ref[...]
    for a in range(traces_ref.shape[1] // LANES):
        cols = slice(a * LANES, (a + 1) * LANES)
        w = w_ref[:, cols]
        ca = ca_ref[:, a : a + 1]
        sa = sa_ref[:, a : a + 1]
        table[:rows, cols] = (w * (ca * cb - sa * sb)).astype(jnp.bfloat16)
        table[rows:, cols] = (-w * (sa * cb + ca * sb)).astype(jnp.bfloat16)
    products = dot_nt(table[...], traces_ref[...])
    real_part = products[:rows]
    imag_part = products[rows:]
    logs = jnp.log(real_part * real_part + imag_part * imag_part + FLOOR)
    out_ref[...] = logs.astype(jnp.bfloat16).reshape(out_ref.shape)


def log_blocks(traces, n_dev, held, padded):
    tr_dev, samples = traces.shape
    groups = 4 if n_dev % 4 == 0 else 1
    dests = n_dev // groups
    rows = dests * padded
    ca, sa, cb, sb, w = base_angles(samples, n_dev, held, padded)
    part = lambda width: pl.BlockSpec((rows, width), lambda g: (g, 0))
    whole = lambda shape: pl.BlockSpec(shape, lambda g: (0, 0))
    return pl.pallas_call(
        logs_kernel,
        grid=(groups,),
        out_shape=jax.ShapeDtypeStruct((n_dev, padded, tr_dev), jnp.bfloat16),
        in_specs=[
            whole((tr_dev, samples)),
            part(ca.shape[1]),
            part(ca.shape[1]),
            part(LANES),
            part(LANES),
            whole((1, samples)),
        ],
        out_specs=pl.BlockSpec((dests, padded, tr_dev), lambda g: (g, 0, 0)),
        scratch_shapes=[pltpu.VMEM((2 * rows, samples), jnp.bfloat16)],
        compiler_params=pltpu.CompilerParams(vmem_limit_bytes=VMEM_BYTES),
        name="logs",
    )(traces, ca, sa, cb, sb, w)


def one_hot(index, count):
    rows = lax.broadcasted_iota(jnp.int32, (count, index.shape[1]), 0)
    return jnp.where(rows == index, 1.0, 0.0).astype(jnp.bfloat16)


def level_mask(index, levels, rows):
    level = lax.broadcasted_iota(jnp.int32, (levels, rows, index.shape[1]), 0)
    return level == index[None]


def spread(values, mask):
    levels, rows, width = mask.shape
    return jnp.where(mask, values[None], 0.0).astype(jnp.bfloat16).reshape(levels * rows, width)


def split_float(values):
    high = values.astype(jnp.bfloat16)
    low = (values - high.astype(jnp.float32)).astype(jnp.bfloat16)
    return jnp.concatenate([high, low], axis=0)


def sweeps_kernel(
    sizes,
    logs_ref,
    ids_ref,
    rec_owner_ref,
    rec_slot_ref,
    cmp_owner_ref,
    cmp_slot_ref,
    out_ref,
    rec_acc,
    cmp_acc,
    so_acc,
    rec_x,
    cmp_x,
    so_x,
    rec_b,
    cmp_b,
    placed,
):
    n_shot, n_off, shot_dev, held, rec_dev, cmp_dev = sizes
    n_dev, padded, tr_dev = logs_ref.shape
    tr_off = tr_dev // shot_dev
    n_bins = n_off * OFFB_DEV
    rec_l = rec_acc.shape[0] // padded
    cmp_l = cmp_acc.shape[0] // padded
    so_width = so_acc.shape[1]
    freq_row = lax.broadcasted_iota(jnp.int32, (padded, tr_dev), 0)
    local_shot = lax.broadcasted_iota(jnp.int32, (1, tr_dev), 1) // tr_off

    def sums_over_traces(first):
        rec_acc[...] = jnp.zeros_like(rec_acc)
        cmp_acc[...] = jnp.zeros_like(cmp_acc)
        so_acc[...] = jnp.zeros_like(so_acc)

        @pl.loop(0, n_dev)
        def _(src):
            ids = ids_ref[src]
            rec = ids[1:2]
            cmp = ids[2:3]
            shot = (src // n_off) * shot_dev + local_shot + n_bins
            so_row = lax.broadcasted_iota(jnp.int32, (so_width, tr_dev), 0)
            so_hot = jnp.where((so_row == ids[0:1]) | (so_row == shot), 1.0, 0.0).astype(
                jnp.bfloat16
            )
            rec_hot = one_hot(rec % WIDE, WIDE)
            cmp_hot = one_hot(cmp % WIDE, WIDE)
            rec_mask = level_mask(rec // WIDE, rec_l, padded)
            cmp_mask = level_mask(cmp // WIDE, cmp_l, padded)
            values = logs_ref[src].astype(jnp.float32)
            if first:
                values = jnp.where(freq_row == held, 1.0, values)
            else:
                so_part = dot_nn(so_x[...], so_hot)
                rec_part = dot_nn(rec_x[...], rec_hot).reshape(rec_mask.shape)
                cmp_part = dot_nn(cmp_x[...], cmp_hot).reshape(cmp_mask.shape)
                values = values - (so_part[:padded] + so_part[padded:])
                values = values - jnp.sum(jnp.where(rec_mask, rec_part, 0.0), axis=0)
                values = values - jnp.sum(jnp.where(cmp_mask, cmp_part, 0.0), axis=0)
            rec_acc[...] += dot_nt(spread(values, rec_mask), rec_hot)
            cmp_acc[...] += dot_nt(spread(values, cmp_mask), cmp_hot)
            so_sums = dot_nt(split_float(values), so_hot)
            so_acc[...] += so_sums[:padded] + so_sums[padded:]

    def update(sums, counts, levels):
        shaped = sums.reshape(levels, padded, sums.shape[1])
        number = counts.reshape(shaped.shape)[:, held : held + 1, :]
        return OMEGA * shaped / (number + 1.0)

    sums_over_traces(True)
    rec_counts, cmp_counts, so_counts = rec_b, cmp_b, placed
    rec_counts[...] = rec_acc[...]
    cmp_counts[...] = cmp_acc[...]
    so_first = update(so_acc[...], so_acc[...], 1).reshape(padded, so_width)
    so_number = so_acc[held : held + 1, :]
    rec_x[...] = update(rec_acc[...], rec_acc[...], rec_l).reshape(rec_x.shape).astype(jnp.bfloat16)
    cmp_x[...] = update(cmp_acc[...], cmp_acc[...], cmp_l).reshape(cmp_x.shape).astype(jnp.bfloat16)
    so_x[...] = split_float(so_first)
    for _ in range(SWEEPS - 1):
        sums_over_traces(False)
    rec_acc[...] = update(rec_acc[...] + rec_counts[...], rec_counts[...], rec_l).reshape(
        rec_acc.shape
    )
    cmp_acc[...] = update(cmp_acc[...] + cmp_counts[...], cmp_counts[...], cmp_l).reshape(
        cmp_acc.shape
    )
    so_final = so_first + OMEGA * so_acc[...] / (so_number + 1.0)

    rec_rows = rec_dev // n_off
    cmp_rows = cmp_dev // n_off
    columns = out_ref.shape[2]
    placed[...] = jnp.zeros_like(placed)

    def place(values, dest, column):
        mask = level_mask(dest, n_dev, padded)
        placed[...] += dot_nt(spread(values, mask), one_hot(column, columns))

    @pl.loop(0, rec_l)
    def _(level):
        position = rec_owner_ref[pl.ds(level, 1)] * rec_dev + rec_slot_ref[pl.ds(level, 1)]
        values = rec_acc[pl.ds(pl.multiple_of(level * padded, 8), padded), :]
        place(values, position // rec_rows, position % rec_rows)

    @pl.loop(0, cmp_l)
    def _(level):
        position = cmp_owner_ref[pl.ds(level, 1)] * cmp_dev + cmp_slot_ref[pl.ds(level, 1)]
        values = cmp_acc[pl.ds(pl.multiple_of(level * padded, 8), padded), :]
        place(values, position // cmp_rows, position % cmp_rows + rec_rows)

    item = lax.broadcasted_iota(jnp.int32, (1, so_width), 1)
    shot = item - n_bins
    is_bin = item < n_bins
    base = rec_rows + cmp_rows
    column = jnp.where(is_bin, base + item % OFFB_DEV, base + OFFB_DEV + shot % shot_dev)
    dest = lax.broadcasted_iota(jnp.int32, (n_dev, padded, so_width), 0)
    items = lax.broadcasted_iota(jnp.int32, (n_dev, padded, so_width), 2)
    mask = jnp.where(items < n_bins, dest % n_off, dest // n_off) == jnp.where(
        items < n_bins, items // OFFB_DEV, (items - n_bins) // shot_dev
    )
    placed[...] += dot_nt(spread(so_final, mask), one_hot(column, columns))
    out_ref[...] = placed[...].astype(jnp.bfloat16).reshape(out_ref.shape)


def run_sweeps(logs, ids, rec_owner, rec_slot, cmp_owner, cmp_slot, sizes, columns):
    n_shot, n_off, shot_dev, _, _, _ = sizes
    n_dev, padded, _ = logs.shape
    rec_l = rec_owner.shape[0]
    cmp_l = cmp_owner.shape[0]
    so_width = up(n_shot * shot_dev + n_off * OFFB_DEV, LANES)
    return pl.pallas_call(
        lambda *refs: sweeps_kernel(sizes, *refs),
        out_shape=jax.ShapeDtypeStruct((n_dev, padded, columns), jnp.bfloat16),
        in_specs=[pl.BlockSpec(memory_space=pltpu.VMEM)] * 6,
        out_specs=pl.BlockSpec(memory_space=pltpu.VMEM),
        scratch_shapes=[
            pltpu.VMEM((rec_l * padded, WIDE), jnp.float32),
            pltpu.VMEM((cmp_l * padded, WIDE), jnp.float32),
            pltpu.VMEM((padded, so_width), jnp.float32),
            pltpu.VMEM((rec_l * padded, WIDE), jnp.bfloat16),
            pltpu.VMEM((cmp_l * padded, WIDE), jnp.bfloat16),
            pltpu.VMEM((2 * padded, so_width), jnp.bfloat16),
            pltpu.VMEM((rec_l * padded, WIDE), jnp.float32),
            pltpu.VMEM((cmp_l * padded, WIDE), jnp.float32),
            pltpu.VMEM((n_dev * padded, columns), jnp.float32),
        ],
        compiler_params=pltpu.CompilerParams(vmem_limit_bytes=VMEM_BYTES),
        name="sweeps",
    )(logs, ids, rec_owner, rec_slot, cmp_owner, cmp_slot)


def shards(traces, offset_bin, rec_id, cmp_id, rec_owner, rec_slot, cmp_owner, cmp_slot):
    shot_dev, tr_off, samples = traces.shape
    n_shot = lax.axis_size("shot")
    n_off = lax.axis_size("off")
    n_dev = n_shot * n_off
    axes = ("shot", "off")
    tr_dev = shot_dev * tr_off
    rec_dev = rec_owner.shape[0] // n_shot
    cmp_dev = cmp_owner.shape[0] // n_shot
    rec_rows = rec_dev // n_off
    cmp_rows = cmp_dev // n_off
    held = up(NF, n_dev) // n_dev
    padded = up(held + 1, 8)
    columns = up(rec_rows + cmp_rows + shot_dev + OFFB_DEV, LANES)
    local_ids = jnp.stack(
        [offset_bin.reshape(tr_dev), rec_id.reshape(tr_dev), cmp_id.reshape(tr_dev)]
    )
    ids = lax.all_gather(local_ids, axes, axis=0)
    blocks = log_blocks(traces.reshape(tr_dev, samples), n_dev, held, padded)
    logs = lax.all_to_all(blocks, axes, split_axis=0, concat_axis=0, tiled=True)
    sizes = (n_shot, n_off, shot_dev, held, rec_dev, cmp_dev)
    wide = lambda table: table.reshape(-1, WIDE)
    terms = run_sweeps(
        logs, ids, wide(rec_owner), wide(rec_slot), wide(cmp_owner), wide(cmp_slot), sizes, columns
    )
    parts = lax.all_to_all(terms, axes, split_axis=0, concat_axis=0, tiled=True)
    held_rows = parts[:, :held].reshape(n_dev * held, columns)[:NF]
    rows = held_rows.astype(jnp.float32).T
    base = rec_rows + cmp_rows
    return (
        rows[base + OFFB_DEV : base + OFFB_DEV + shot_dev],
        rows[base : base + OFFB_DEV],
        rows[:rec_rows],
        rows[rec_rows:base],
    )


def solution(mesh):
    return jax.shard_map(
        shards,
        mesh=mesh,
        in_specs=(
            P("shot", "off", None),
            P("shot", "off"),
            P("shot", "off"),
            P("shot", "off"),
            P(),
            P(),
            P(),
            P(),
        ),
        out_specs=(
            P("shot", None),
            P("off", None),
            P(("shot", "off"), None),
            P(("shot", "off"), None),
        ),
        check_vma=False,
    )
```

```python
import math

import jax
import jax.numpy as jnp
import numpy as np
from jax import lax
from jax.experimental import pallas as pl
from jax.experimental.pallas import tpu as pltpu
from jax.sharding import PartitionSpec as P

NF = 640
OFFB_DEV = 8
SWEEPS = 2
LANES = 128
WIDE = 256

OMEGA = 0.35
FLOOR = 0.05
VMEM_BYTES = 60 * 1024 * 1024


def up(value, unit):
    return -(-value // unit) * unit


def dot_nt(a, b):
    return lax.dot_general(a, b, (((1,), (1,)), ((), ())), preferred_element_type=jnp.float32)


def dot_nn(a, b):
    return lax.dot_general(a, b, (((1,), (0,)), ((), ())), preferred_element_type=jnp.float32)


def base_angles(samples, n_dev, held, padded):
    row = np.arange(n_dev * padded)
    freq = ((row // padded) * held + row % padded)[:, None]
    step = 2.0 * math.pi / samples
    coarse = freq * (np.arange(samples // LANES)[None, :] * LANES) % samples * step
    fine = freq * np.arange(LANES)[None, :] % samples * step
    tapers = 0.5 - 0.5 * np.cos((np.arange(samples)[None, :] + 0.5) * step)
    weights = tapers * math.sqrt(8.0 / (3.0 * samples))
    tables = (np.cos(coarse), np.sin(coarse), np.cos(fine), np.sin(fine), weights)
    return tuple(table.astype(np.float32) for table in tables)


def my_position(n_off):
    return lax.axis_index("shot") * n_off + lax.axis_index("off")


def remote(src, dst, send_sem, recv_sem, dest, n_off):
    return pltpu.make_async_remote_copy(
        src_ref=src,
        dst_ref=dst,
        send_sem=send_sem,
        recv_sem=recv_sem,
        device_id=(dest // n_off, dest % n_off),
        device_id_type=pl.DeviceIdType.MESH,
    )


def greet_all(me, n_dev, n_off):
    barrier = pltpu.get_barrier_semaphore()

    @pl.loop(1, n_dev)
    def _(step):
        dest = (me + step) % n_dev
        pl.semaphore_signal(
            barrier,
            inc=1,
            device_id=(dest // n_off, dest % n_off),
            device_id_type=pl.DeviceIdType.MESH,
        )

    return barrier


def logs_kernel(
    n_off,
    groups,
    traces_ref,
    ids_ref,
    ca_ref,
    sa_ref,
    cb_ref,
    sb_ref,
    w_ref,
    out_ref,
    ids_out_ref,
    stage,
    table,
    send_sems,
    recv_sems,
    id_send_sems,
    id_recv_sems,
    own_sems,
):
    n_dev, padded, tr_dev = out_ref.shape
    dests = n_dev // groups
    rows = dests * padded
    me = my_position(n_off)
    barrier = greet_all(me, n_dev, n_off)

    def block_copy(dest, slot):
        return remote(
            stage.at[dest], out_ref.at[slot], send_sems.at[dest], recv_sems.at[slot], dest, n_off
        )

    def id_copy(dest, slot):
        return remote(
            ids_ref, ids_out_ref.at[slot], id_send_sems.at[dest], id_recv_sems.at[slot], dest, n_off
        )

    own_ids = pltpu.make_async_copy(ids_ref, ids_out_ref.at[me], own_sems.at[0])
    own_ids.start()
    for turn in range(groups):
        group = ((me // dests) + groups - 1 - turn) % groups
        if groups & (groups - 1) == 0:
            group = (me // dests) ^ (groups - 1 - turn)
        base = pl.multiple_of(group * rows, 8)
        cb = cb_ref[pl.ds(base, rows), :]
        sb = sb_ref[pl.ds(base, rows), :]
        ca_all = ca_ref[pl.ds(base, rows), :]
        sa_all = sa_ref[pl.ds(base, rows), :]
        for a in range(traces_ref.shape[1] // LANES):
            cols = slice(a * LANES, (a + 1) * LANES)
            w = w_ref[:, cols]
            ca = ca_all[:, a : a + 1]
            sa = sa_all[:, a : a + 1]
            table[:rows, cols] = (w * (ca * cb - sa * sb)).astype(jnp.bfloat16)
            table[rows:, cols] = (-w * (sa * cb + ca * sb)).astype(jnp.bfloat16)
        products = dot_nt(table[...], traces_ref[...])
        real_part = products[:rows]
        imag_part = products[rows:]
        logs = jnp.log(real_part * real_part + imag_part * imag_part + FLOOR)
        stage[pl.ds(group * dests, dests)] = logs.astype(jnp.bfloat16).reshape(
            dests, padded, tr_dev
        )
        if turn == 0:
            pl.semaphore_wait(barrier, n_dev - 1)

        @pl.loop(0, dests)
        def _(step):
            dest = group * dests + (step + me) % dests

            @pl.when(dest != me)
            def _():
                block_copy(dest, me).start()

        if turn == 0:

            @pl.loop(1, n_dev)
            def _(step):
                id_copy((me + step) % n_dev, me).start()

    own = pltpu.make_async_copy(stage.at[me], out_ref.at[me], own_sems.at[1])
    own.start()

    @pl.loop(1, n_dev)
    def _(step):
        dest = (me + step) % n_dev
        block_copy(dest, me).wait_send()
        id_copy(dest, me).wait_send()
        block_copy(dest, dest).wait_recv()
        id_copy(dest, dest).wait_recv()

    own.wait()
    own_ids.wait()


def log_blocks(traces, ids, n_off, n_dev, held, padded):
    tr_dev, samples = traces.shape
    groups = 4 if n_dev % 4 == 0 else 1
    rows = n_dev // groups * padded
    tables = base_angles(samples, n_dev, held, padded)
    vmem = pl.BlockSpec(memory_space=pltpu.VMEM)
    return pl.pallas_call(
        lambda *refs: logs_kernel(n_off, groups, *refs),
        out_shape=(
            jax.ShapeDtypeStruct((n_dev, padded, tr_dev), jnp.bfloat16),
            jax.ShapeDtypeStruct((n_dev,) + ids.shape, ids.dtype),
        ),
        in_specs=[vmem] * 7,
        out_specs=(vmem, vmem),
        scratch_shapes=[
            pltpu.VMEM((n_dev, padded, tr_dev), jnp.bfloat16),
            pltpu.VMEM((2 * rows, samples), jnp.bfloat16),
            pltpu.SemaphoreType.DMA((n_dev,)),
            pltpu.SemaphoreType.DMA((n_dev,)),
            pltpu.SemaphoreType.DMA((n_dev,)),
            pltpu.SemaphoreType.DMA((n_dev,)),
            pltpu.SemaphoreType.DMA((2,)),
        ],
        compiler_params=pltpu.CompilerParams(
            vmem_limit_bytes=VMEM_BYTES, collective_id=0, has_side_effects=True
        ),
        name="logs",
    )(traces, ids, *tables)


def return_kernel(
    n_off,
    splits,
    terms_ref,
    source_ref,
    offset_ref,
    rec_ref,
    cmp_ref,
    landed,
    joined,
    send_sems,
    recv_sems,
    own_sem,
):
    n_dev = terms_ref.shape[0]
    held = -(-source_ref.shape[1] // n_dev)
    me = my_position(n_off)
    barrier = greet_all(me, n_dev, n_off)

    def block_copy(dest, slot):
        return remote(
            terms_ref.at[dest], landed.at[slot], send_sems.at[dest], recv_sems.at[slot], dest, n_off
        )

    own = pltpu.make_async_copy(terms_ref.at[me], landed.at[me], own_sem)
    own.start()
    pl.semaphore_wait(barrier, n_dev - 1)

    @pl.loop(1, n_dev)
    def _(step):
        block_copy((me + step) % n_dev, me).start()

    @pl.loop(1, n_dev)
    def _(step):
        dest = (me + step) % n_dev
        block_copy(dest, me).wait_send()
        block_copy(dest, dest).wait_recv()

    own.wait()
    for src in range(n_dev):
        rows = min(held, joined.shape[0] - src * held)
        if rows > 0:
            joined[src * held : src * held + rows, :] = landed[src].astype(jnp.float32)[:rows]
    turned = joined[...].T
    a, b, c, d = splits
    rec_ref[...] = turned[:a]
    cmp_ref[...] = turned[a:b]
    offset_ref[...] = turned[b:c]
    source_ref[...] = turned[c:d]


def return_terms(terms, n_off, splits):
    n_dev, padded, columns = terms.shape
    a, b, c, d = splits
    vmem = pl.BlockSpec(memory_space=pltpu.VMEM)
    shape = lambda rows: jax.ShapeDtypeStruct((rows, NF), jnp.float32)
    return pl.pallas_call(
        lambda *refs: return_kernel(n_off, splits, *refs),
        out_shape=(shape(d - c), shape(c - b), shape(a), shape(b - a)),
        in_specs=[vmem],
        out_specs=(vmem,) * 4,
        scratch_shapes=[
            pltpu.VMEM((n_dev, padded, columns), jnp.bfloat16),
            pltpu.VMEM((NF, columns), jnp.float32),
            pltpu.SemaphoreType.DMA((n_dev,)),
            pltpu.SemaphoreType.DMA((n_dev,)),
            pltpu.SemaphoreType.DMA,
        ],
        compiler_params=pltpu.CompilerParams(
            vmem_limit_bytes=VMEM_BYTES, collective_id=1, has_side_effects=True
        ),
        name="returns",
    )(terms)


def one_hot(index, count):
    rows = lax.broadcasted_iota(jnp.int32, (count, index.shape[1]), 0)
    return jnp.where(rows == index, 1.0, 0.0).astype(jnp.bfloat16)


def level_mask(index, levels, rows):
    level = lax.broadcasted_iota(jnp.int32, (levels, rows, index.shape[1]), 0)
    return level == index[None]


def spread(values, mask):
    levels, rows, width = mask.shape
    return jnp.where(mask, values[None], 0.0).astype(jnp.bfloat16).reshape(levels * rows, width)


def split_float(values):
    high = values.astype(jnp.bfloat16)
    low = (values - high.astype(jnp.float32)).astype(jnp.bfloat16)
    return jnp.concatenate([high, low], axis=0)


def sweeps_kernel(
    sizes,
    logs_ref,
    ids_ref,
    rec_owner_ref,
    rec_slot_ref,
    cmp_owner_ref,
    cmp_slot_ref,
    out_ref,
    rec_acc,
    cmp_acc,
    so_acc,
    rec_x,
    cmp_x,
    so_x,
    rec_b,
    cmp_b,
    placed,
):
    n_shot, n_off, shot_dev, held, rec_dev, cmp_dev = sizes
    n_dev, padded, tr_dev = logs_ref.shape
    tr_off = tr_dev // shot_dev
    n_bins = n_off * OFFB_DEV
    rec_l = rec_acc.shape[0] // padded
    cmp_l = cmp_acc.shape[0] // padded
    so_width = so_acc.shape[1]
    freq_row = lax.broadcasted_iota(jnp.int32, (padded, tr_dev), 0)
    local_shot = lax.broadcasted_iota(jnp.int32, (1, tr_dev), 1) // tr_off

    def sums_over_traces(first):
        rec_acc[...] = jnp.zeros_like(rec_acc)
        cmp_acc[...] = jnp.zeros_like(cmp_acc)
        so_acc[...] = jnp.zeros_like(so_acc)

        @pl.loop(0, n_dev)
        def _(src):
            ids = ids_ref[src]
            rec = ids[1:2]
            cmp = ids[2:3]
            shot = (src // n_off) * shot_dev + local_shot + n_bins
            so_row = lax.broadcasted_iota(jnp.int32, (so_width, tr_dev), 0)
            so_hot = jnp.where((so_row == ids[0:1]) | (so_row == shot), 1.0, 0.0).astype(
                jnp.bfloat16
            )
            rec_hot = one_hot(rec % WIDE, WIDE)
            cmp_hot = one_hot(cmp % WIDE, WIDE)
            rec_mask = level_mask(rec // WIDE, rec_l, padded)
            cmp_mask = level_mask(cmp // WIDE, cmp_l, padded)
            values = logs_ref[src].astype(jnp.float32)
            if first:
                values = jnp.where(freq_row == held, 1.0, values)
            else:
                so_part = dot_nn(so_x[...], so_hot)
                rec_part = dot_nn(rec_x[...], rec_hot).reshape(rec_mask.shape)
                cmp_part = dot_nn(cmp_x[...], cmp_hot).reshape(cmp_mask.shape)
                values = values - (so_part[:padded] + so_part[padded:])
                values = values - jnp.sum(jnp.where(rec_mask, rec_part, 0.0), axis=0)
                values = values - jnp.sum(jnp.where(cmp_mask, cmp_part, 0.0), axis=0)
            rec_acc[...] += dot_nt(spread(values, rec_mask), rec_hot)
            cmp_acc[...] += dot_nt(spread(values, cmp_mask), cmp_hot)
            so_sums = dot_nt(split_float(values), so_hot)
            so_acc[...] += so_sums[:padded] + so_sums[padded:]

    def update(sums, counts, levels):
        shaped = sums.reshape(levels, padded, sums.shape[1])
        number = counts.reshape(shaped.shape)[:, held : held + 1, :]
        return OMEGA * shaped / (number + 1.0)

    sums_over_traces(True)
    rec_counts, cmp_counts, so_counts = rec_b, cmp_b, placed
    rec_counts[...] = rec_acc[...]
    cmp_counts[...] = cmp_acc[...]
    so_first = update(so_acc[...], so_acc[...], 1).reshape(padded, so_width)
    so_number = so_acc[held : held + 1, :]
    rec_x[...] = update(rec_acc[...], rec_acc[...], rec_l).reshape(rec_x.shape).astype(jnp.bfloat16)
    cmp_x[...] = update(cmp_acc[...], cmp_acc[...], cmp_l).reshape(cmp_x.shape).astype(jnp.bfloat16)
    so_x[...] = split_float(so_first)
    for _ in range(SWEEPS - 1):
        sums_over_traces(False)
    rec_acc[...] = update(rec_acc[...] + rec_counts[...], rec_counts[...], rec_l).reshape(
        rec_acc.shape
    )
    cmp_acc[...] = update(cmp_acc[...] + cmp_counts[...], cmp_counts[...], cmp_l).reshape(
        cmp_acc.shape
    )
    so_final = so_first + OMEGA * so_acc[...] / (so_number + 1.0)

    rec_rows = rec_dev // n_off
    cmp_rows = cmp_dev // n_off
    columns = out_ref.shape[2]
    placed[...] = jnp.zeros_like(placed)

    def place(values, dest, column):
        mask = level_mask(dest, n_dev, padded)
        placed[...] += dot_nt(spread(values, mask), one_hot(column, columns))

    @pl.loop(0, rec_l)
    def _(level):
        position = rec_owner_ref[pl.ds(level, 1)] * rec_dev + rec_slot_ref[pl.ds(level, 1)]
        values = rec_acc[pl.ds(pl.multiple_of(level * padded, 8), padded), :]
        place(values, position // rec_rows, position % rec_rows)

    @pl.loop(0, cmp_l)
    def _(level):
        position = cmp_owner_ref[pl.ds(level, 1)] * cmp_dev + cmp_slot_ref[pl.ds(level, 1)]
        values = cmp_acc[pl.ds(pl.multiple_of(level * padded, 8), padded), :]
        place(values, position // cmp_rows, position % cmp_rows + rec_rows)

    item = lax.broadcasted_iota(jnp.int32, (1, so_width), 1)
    shot = item - n_bins
    is_bin = item < n_bins
    base = rec_rows + cmp_rows
    column = jnp.where(is_bin, base + item % OFFB_DEV, base + OFFB_DEV + shot % shot_dev)
    dest = lax.broadcasted_iota(jnp.int32, (n_dev, padded, so_width), 0)
    items = lax.broadcasted_iota(jnp.int32, (n_dev, padded, so_width), 2)
    mask = jnp.where(items < n_bins, dest % n_off, dest // n_off) == jnp.where(
        items < n_bins, items // OFFB_DEV, (items - n_bins) // shot_dev
    )
    placed[...] += dot_nt(spread(so_final, mask), one_hot(column, columns))
    out_ref[...] = placed[...].astype(jnp.bfloat16).reshape(out_ref.shape)


def run_sweeps(logs, ids, rec_owner, rec_slot, cmp_owner, cmp_slot, sizes, columns):
    n_shot, n_off, shot_dev, _, _, _ = sizes
    n_dev, padded, _ = logs.shape
    rec_l = rec_owner.shape[0]
    cmp_l = cmp_owner.shape[0]
    so_width = up(n_shot * shot_dev + n_off * OFFB_DEV, LANES)
    return pl.pallas_call(
        lambda *refs: sweeps_kernel(sizes, *refs),
        out_shape=jax.ShapeDtypeStruct((n_dev, padded, columns), jnp.bfloat16),
        in_specs=[pl.BlockSpec(memory_space=pltpu.VMEM)] * 6,
        out_specs=pl.BlockSpec(memory_space=pltpu.VMEM),
        scratch_shapes=[
            pltpu.VMEM((rec_l * padded, WIDE), jnp.float32),
            pltpu.VMEM((cmp_l * padded, WIDE), jnp.float32),
            pltpu.VMEM((padded, so_width), jnp.float32),
            pltpu.VMEM((rec_l * padded, WIDE), jnp.bfloat16),
            pltpu.VMEM((cmp_l * padded, WIDE), jnp.bfloat16),
            pltpu.VMEM((2 * padded, so_width), jnp.bfloat16),
            pltpu.VMEM((rec_l * padded, WIDE), jnp.float32),
            pltpu.VMEM((cmp_l * padded, WIDE), jnp.float32),
            pltpu.VMEM((n_dev * padded, columns), jnp.float32),
        ],
        compiler_params=pltpu.CompilerParams(vmem_limit_bytes=VMEM_BYTES),
        name="sweeps",
    )(logs, ids, rec_owner, rec_slot, cmp_owner, cmp_slot)


def shards(traces, offset_bin, rec_id, cmp_id, rec_owner, rec_slot, cmp_owner, cmp_slot):
    shot_dev, tr_off, samples = traces.shape
    n_shot = lax.axis_size("shot")
    n_off = lax.axis_size("off")
    n_dev = n_shot * n_off
    tr_dev = shot_dev * tr_off
    rec_dev = rec_owner.shape[0] // n_shot
    cmp_dev = cmp_owner.shape[0] // n_shot
    rec_rows = rec_dev // n_off
    cmp_rows = cmp_dev // n_off
    held = up(NF, n_dev) // n_dev
    padded = up(held + 1, 8)
    columns = up(rec_rows + cmp_rows + shot_dev + OFFB_DEV, LANES)
    local_ids = jnp.stack(
        [offset_bin.reshape(tr_dev), rec_id.reshape(tr_dev), cmp_id.reshape(tr_dev)]
    )
    logs, ids = log_blocks(
        traces.reshape(tr_dev, samples), local_ids, n_off, n_dev, held, padded
    )
    sizes = (n_shot, n_off, shot_dev, held, rec_dev, cmp_dev)
    wide = lambda table: table.reshape(-1, WIDE)
    terms = run_sweeps(
        logs, ids, wide(rec_owner), wide(rec_slot), wide(cmp_owner), wide(cmp_slot), sizes, columns
    )
    base = rec_rows + cmp_rows
    splits = (rec_rows, base, base + OFFB_DEV, base + OFFB_DEV + shot_dev)
    return return_terms(terms, n_off, splits)


def solution(mesh):
    return jax.shard_map(
        shards,
        mesh=mesh,
        in_specs=(
            P("shot", "off", None),
            P("shot", "off"),
            P("shot", "off"),
            P("shot", "off"),
            P(),
            P(),
            P(),
            P(),
        ),
        out_specs=(
            P("shot", None),
            P("off", None),
            P(("shot", "off"), None),
            P(("shot", "off"), None),
        ),
        check_vma=False,
    )
```

```python
import math

import jax
import jax.numpy as jnp
import numpy as np
from jax import lax
from jax.experimental import pallas as pl
from jax.experimental.pallas import tpu as pltpu
from jax.sharding import PartitionSpec as P

NF = 640
OFFB_DEV = 8
SWEEPS = 2
LANES = 128
WIDE = 256

OMEGA = 0.35
FLOOR = 0.05
VMEM_BYTES = 60 * 1024 * 1024


def up(value, unit):
    return -(-value // unit) * unit


def dot_nt(a, b):
    return lax.dot_general(a, b, (((1,), (1,)), ((), ())), preferred_element_type=jnp.float32)


def dot_nn(a, b):
    return lax.dot_general(a, b, (((1,), (0,)), ((), ())), preferred_element_type=jnp.float32)


def base_angles(samples, n_dev, held, padded):
    row = np.arange(n_dev * padded)
    freq = ((row // padded) * held + row % padded)[:, None]
    step = 2.0 * math.pi / samples
    coarse = freq * (np.arange(samples // LANES)[None, :] * LANES) % samples * step
    fine = freq * np.arange(LANES)[None, :] % samples * step
    tapers = 0.5 - 0.5 * np.cos((np.arange(samples)[None, :] + 0.5) * step)
    weights = tapers * math.sqrt(8.0 / (3.0 * samples))
    tables = (np.cos(coarse), np.sin(coarse), np.cos(fine), np.sin(fine), weights)
    return tuple(table.astype(np.float32) for table in tables)


def my_position(n_off):
    return lax.axis_index("shot") * n_off + lax.axis_index("off")


def remote(src, dst, send_sem, recv_sem, dest, n_off):
    return pltpu.make_async_remote_copy(
        src_ref=src,
        dst_ref=dst,
        send_sem=send_sem,
        recv_sem=recv_sem,
        device_id=(dest // n_off, dest % n_off),
        device_id_type=pl.DeviceIdType.MESH,
    )


def greet_all(me, n_dev, n_off):
    barrier = pltpu.get_barrier_semaphore()

    @pl.loop(1, n_dev)
    def _(step):
        dest = (me + step) % n_dev
        pl.semaphore_signal(
            barrier,
            inc=1,
            device_id=(dest // n_off, dest % n_off),
            device_id_type=pl.DeviceIdType.MESH,
        )

    return barrier


def send_logs(n_off, groups, held, traces_ref, id_refs, table_refs, landed, bins, scratch):
    ca_ref, sa_ref, cb_ref, sb_ref, w_ref = table_refs
    stage, own_bins, id_rows, table, send_sems, recv_sems, bin_send_sems, bin_recv_sems, own_sems = (
        scratch
    )
    n_dev, padded, tr_dev = landed.shape
    dests = n_dev // groups
    rows = dests * padded
    me = my_position(n_off)
    barrier = greet_all(me, n_dev, n_off)
    bin_ref, rec_ref, cmp_ref = id_refs
    shot_dev, tr_off = bin_ref.shape
    id_rows[...] = jnp.zeros_like(id_rows)
    for shot in range(shot_dev):
        cols = slice(shot * tr_off, (shot + 1) * tr_off)
        own_bins[:, cols] = bin_ref[shot : shot + 1, :]
        rec = rec_ref[shot : shot + 1, :]
        cmp = cmp_ref[shot : shot + 1, :]
        parts = (rec % WIDE, rec // WIDE, cmp % WIDE, cmp // WIDE)
        for k, part in enumerate(parts):
            id_rows[held + k : held + k + 1, cols] = part.astype(jnp.float32)

    def block_copy(dest, slot):
        return remote(
            stage.at[dest], landed.at[slot], send_sems.at[dest], recv_sems.at[slot], dest, n_off
        )

    def bin_copy(dest, slot):
        return remote(
            own_bins, bins.at[slot], bin_send_sems.at[dest], bin_recv_sems.at[slot], dest, n_off
        )

    def turn_group(turn):
        if groups & (groups - 1) == 0:
            return (me // dests) ^ (groups - 1 - turn)
        return ((me // dests) + groups - 1 - turn) % groups

    own_copy = pltpu.make_async_copy(own_bins, bins.at[me], own_sems.at[0])
    own_copy.start()
    freq_row = lax.broadcasted_iota(jnp.int32, (dests, padded, tr_dev), 1)
    for turn in range(groups):
        group = turn_group(turn)
        base = pl.multiple_of(group * rows, 8)
        cb = cb_ref[pl.ds(base, rows), :]
        sb = sb_ref[pl.ds(base, rows), :]
        ca_all = ca_ref[pl.ds(base, rows), :]
        sa_all = sa_ref[pl.ds(base, rows), :]
        for a in range(traces_ref.shape[1] // LANES):
            cols = slice(a * LANES, (a + 1) * LANES)
            w = w_ref[:, cols]
            ca = ca_all[:, a : a + 1]
            sa = sa_all[:, a : a + 1]
            table[:rows, cols] = (w * (ca * cb - sa * sb)).astype(jnp.bfloat16)
            table[rows:, cols] = (-w * (sa * cb + ca * sb)).astype(jnp.bfloat16)
        products = dot_nt(table[...], traces_ref[...])
        real_part = products[:rows]
        imag_part = products[rows:]
        logs = jnp.log(real_part * real_part + imag_part * imag_part + FLOOR)
        logs = logs.reshape(dests, padded, tr_dev)
        logs = jnp.where(freq_row < held, logs, id_rows[...][None])
        stage[pl.ds(group * dests, dests)] = logs.astype(jnp.bfloat16)
        if turn == 0:
            pl.semaphore_wait(barrier, n_dev - 1)

        @pl.loop(0, dests)
        def _(step):
            dest = group * dests + (step + me) % dests

            @pl.when(dest != me)
            def _():
                block_copy(dest, me).start()
                bin_copy(dest, me).start()

    own = pltpu.make_async_copy(stage.at[me], landed.at[me], own_sems.at[1])
    own.start()
    own_copy.wait()
    own.wait()

    def arrival(turn, step):
        src = turn_group(turn) * dests + (me + dests - step) % dests

        @pl.when(src != me)
        def _():
            block_copy(src, src).wait_recv()
            bin_copy(src, src).wait_recv()

        return src

    def finish():
        @pl.loop(1, n_dev)
        def _(step):
            dest = (me + step) % n_dev
            block_copy(dest, me).wait_send()
            bin_copy(dest, me).wait_send()

    return arrival, finish


def return_kernel(
    n_off,
    splits,
    terms_ref,
    source_ref,
    offset_ref,
    rec_ref,
    cmp_ref,
    landed,
    joined,
    send_sems,
    recv_sems,
    own_sem,
):
    n_dev = terms_ref.shape[0]
    held = -(-source_ref.shape[1] // n_dev)
    me = my_position(n_off)
    barrier = greet_all(me, n_dev, n_off)

    def block_copy(dest, slot):
        return remote(
            terms_ref.at[dest], landed.at[slot], send_sems.at[dest], recv_sems.at[slot], dest, n_off
        )

    own = pltpu.make_async_copy(terms_ref.at[me], landed.at[me], own_sem)
    own.start()
    pl.semaphore_wait(barrier, n_dev - 1)

    @pl.loop(1, n_dev)
    def _(step):
        block_copy((me + step) % n_dev, me).start()

    @pl.loop(1, n_dev)
    def _(step):
        dest = (me + step) % n_dev
        block_copy(dest, me).wait_send()
        block_copy(dest, dest).wait_recv()

    own.wait()
    for src in range(n_dev):
        rows = min(held, joined.shape[0] - src * held)
        if rows > 0:
            joined[src * held : src * held + rows, :] = landed[src].astype(jnp.float32)[:rows]
    turned = joined[...].T
    a, b, c, d = splits
    rec_ref[...] = turned[:a]
    cmp_ref[...] = turned[a:b]
    offset_ref[...] = turned[b:c]
    source_ref[...] = turned[c:d]


def return_terms(terms, n_off, splits):
    n_dev, padded, columns = terms.shape
    a, b, c, d = splits
    vmem = pl.BlockSpec(memory_space=pltpu.VMEM)
    shape = lambda rows: jax.ShapeDtypeStruct((rows, NF), jnp.float32)
    return pl.pallas_call(
        lambda *refs: return_kernel(n_off, splits, *refs),
        out_shape=(shape(d - c), shape(c - b), shape(a), shape(b - a)),
        in_specs=[vmem],
        out_specs=(vmem,) * 4,
        scratch_shapes=[
            pltpu.VMEM((n_dev, padded, columns), jnp.bfloat16),
            pltpu.VMEM((NF, columns), jnp.float32),
            pltpu.SemaphoreType.DMA((n_dev,)),
            pltpu.SemaphoreType.DMA((n_dev,)),
            pltpu.SemaphoreType.DMA,
        ],
        compiler_params=pltpu.CompilerParams(
            vmem_limit_bytes=VMEM_BYTES, collective_id=1, has_side_effects=True
        ),
        name="returns",
    )(terms)


def one_hot(index, count):
    rows = lax.broadcasted_iota(jnp.int32, (count, index.shape[1]), 0)
    return jnp.where(rows.astype(index.dtype) == index, 1.0, 0.0).astype(jnp.bfloat16)


def level_mask(index, levels, rows):
    level = lax.broadcasted_iota(jnp.int32, (levels, rows, index.shape[1]), 0)
    return level.astype(index.dtype) == index[None]


def spread(values, mask):
    levels, rows, width = mask.shape
    return jnp.where(mask, values[None], 0.0).astype(jnp.bfloat16).reshape(levels * rows, width)


def split_float(values):
    high = values.astype(jnp.bfloat16)
    low = (values - high.astype(jnp.float32)).astype(jnp.bfloat16)
    return jnp.concatenate([high, low], axis=0)


def sweeps_kernel(
    sizes,
    traces_ref,
    bin_ref,
    rec_ref,
    cmp_ref,
    ca_ref,
    sa_ref,
    cb_ref,
    sb_ref,
    w_ref,
    rec_owner_ref,
    rec_slot_ref,
    cmp_owner_ref,
    cmp_slot_ref,
    out_ref,
    landed,
    bins,
    rec_acc,
    cmp_acc,
    so_acc,
    rec_x,
    cmp_x,
    so_x,
    rec_b,
    cmp_b,
    placed,
    *send_scratch,
):
    n_shot, n_off, shot_dev, held, rec_dev, cmp_dev = sizes
    n_dev, padded, tr_dev = landed.shape
    groups = 4 if n_dev % 4 == 0 else 1
    dests = n_dev // groups
    tr_off = tr_dev // shot_dev
    n_bins = n_off * OFFB_DEV
    rec_l = rec_acc.shape[0] // padded
    cmp_l = cmp_acc.shape[0] // padded
    so_width = so_acc.shape[1]
    freq_row = lax.broadcasted_iota(jnp.int32, (padded, tr_dev), 0)
    local_shot = lax.broadcasted_iota(jnp.int32, (1, tr_dev), 1) // tr_off
    arrival, finish = send_logs(
        n_off,
        groups,
        held,
        traces_ref,
        (bin_ref, rec_ref, cmp_ref),
        (ca_ref, sa_ref, cb_ref, sb_ref, w_ref),
        landed,
        bins,
        send_scratch,
    )

    def add_source(src, first):
        values = landed[src].astype(jnp.float32)
        rec_h, rec_level, cmp_h, cmp_level = (
            values[held + k : held + k + 1] for k in range(4)
        )
        shot = (src // n_off) * shot_dev + local_shot + n_bins
        so_row = lax.broadcasted_iota(jnp.int32, (so_width, tr_dev), 0)
        so_hot = jnp.where((so_row == bins[src]) | (so_row == shot), 1.0, 0.0).astype(jnp.bfloat16)
        rec_hot = one_hot(rec_h, WIDE)
        cmp_hot = one_hot(cmp_h, WIDE)
        rec_mask = level_mask(rec_level, rec_l, padded)
        cmp_mask = level_mask(cmp_level, cmp_l, padded)
        if first:
            values = jnp.where(freq_row == held, 1.0, values)
        else:
            so_part = dot_nn(so_x[...], so_hot)
            rec_part = dot_nn(rec_x[...], rec_hot).reshape(rec_mask.shape)
            cmp_part = dot_nn(cmp_x[...], cmp_hot).reshape(cmp_mask.shape)
            values = values - (so_part[:padded] + so_part[padded:])
            values = values - jnp.sum(jnp.where(rec_mask, rec_part, 0.0), axis=0)
            values = values - jnp.sum(jnp.where(cmp_mask, cmp_part, 0.0), axis=0)
        rec_acc[...] += dot_nt(spread(values, rec_mask), rec_hot)
        cmp_acc[...] += dot_nt(spread(values, cmp_mask), cmp_hot)
        so_acc[...] += dot_nt(values.astype(jnp.bfloat16), so_hot)

    def sums_over_traces(first):
        rec_acc[...] = jnp.zeros_like(rec_acc)
        cmp_acc[...] = jnp.zeros_like(cmp_acc)
        so_acc[...] = jnp.zeros_like(so_acc)
        if not first:

            @pl.loop(0, n_dev)
            def _(src):
                add_source(src, False)

            return
        @pl.loop(0, n_dev)
        def _(step):
            add_source(arrival(step // dests, step % dests), True)

        finish()

    def update(sums, counts, levels):
        shaped = sums.reshape(levels, padded, sums.shape[1])
        number = counts.reshape(shaped.shape)[:, held : held + 1, :]
        return OMEGA * shaped / (number + 1.0)

    sums_over_traces(True)
    rec_counts, cmp_counts, so_counts = rec_b, cmp_b, placed
    rec_counts[...] = rec_acc[...]
    cmp_counts[...] = cmp_acc[...]
    so_first = update(so_acc[...], so_acc[...], 1).reshape(padded, so_width)
    so_number = so_acc[held : held + 1, :]
    rec_x[...] = update(rec_acc[...], rec_acc[...], rec_l).reshape(rec_x.shape).astype(jnp.bfloat16)
    cmp_x[...] = update(cmp_acc[...], cmp_acc[...], cmp_l).reshape(cmp_x.shape).astype(jnp.bfloat16)
    so_x[...] = split_float(so_first)
    for _ in range(SWEEPS - 1):
        sums_over_traces(False)
    rec_acc[...] = update(rec_acc[...] + rec_counts[...], rec_counts[...], rec_l).reshape(
        rec_acc.shape
    )
    cmp_acc[...] = update(cmp_acc[...] + cmp_counts[...], cmp_counts[...], cmp_l).reshape(
        cmp_acc.shape
    )
    so_final = so_first + OMEGA * so_acc[...] / (so_number + 1.0)

    rec_rows = rec_dev // n_off
    cmp_rows = cmp_dev // n_off
    columns = out_ref.shape[2]
    placed[...] = jnp.zeros_like(placed)

    def place(values, dest, column):
        mask = level_mask(dest, n_dev, padded)
        placed[...] += dot_nt(spread(values, mask), one_hot(column, columns))

    @pl.loop(0, rec_l)
    def _(level):
        span = pl.ds(pl.multiple_of(level * WIDE, WIDE), WIDE)
        position = (rec_owner_ref[span] * rec_dev + rec_slot_ref[span]).reshape(1, WIDE)
        values = rec_acc[pl.ds(pl.multiple_of(level * padded, 8), padded), :]
        place(values, position // rec_rows, position % rec_rows)

    @pl.loop(0, cmp_l)
    def _(level):
        span = pl.ds(pl.multiple_of(level * WIDE, WIDE), WIDE)
        position = (cmp_owner_ref[span] * cmp_dev + cmp_slot_ref[span]).reshape(1, WIDE)
        values = cmp_acc[pl.ds(pl.multiple_of(level * padded, 8), padded), :]
        place(values, position // cmp_rows, position % cmp_rows + rec_rows)

    item = lax.broadcasted_iota(jnp.int32, (1, so_width), 1)
    shot = item - n_bins
    is_bin = item < n_bins
    base = rec_rows + cmp_rows
    column = jnp.where(is_bin, base + item % OFFB_DEV, base + OFFB_DEV + shot % shot_dev)
    dest = lax.broadcasted_iota(jnp.int32, (n_dev, padded, so_width), 0)
    items = lax.broadcasted_iota(jnp.int32, (n_dev, padded, so_width), 2)
    mask = jnp.where(items < n_bins, dest % n_off, dest // n_off) == jnp.where(
        items < n_bins, items // OFFB_DEV, (items - n_bins) // shot_dev
    )
    placed[...] += dot_nt(spread(so_final, mask), one_hot(column, columns))
    out_ref[...] = placed[...].astype(jnp.bfloat16).reshape(out_ref.shape)


def run_sweeps(traces, ids, owners, sizes, padded, columns):
    n_shot, n_off, shot_dev, held, _, _ = sizes
    n_dev = n_shot * n_off
    tr_dev, samples = traces.shape
    groups = 4 if n_dev % 4 == 0 else 1
    rows = n_dev // groups * padded
    rec_l = owners[0].shape[0] // WIDE
    cmp_l = owners[2].shape[0] // WIDE
    so_width = up(n_shot * shot_dev + n_off * OFFB_DEV, LANES)
    tables = base_angles(samples, n_dev, held, padded)
    vmem = pl.BlockSpec(memory_space=pltpu.VMEM)
    return pl.pallas_call(
        lambda *refs: sweeps_kernel(sizes, *refs),
        out_shape=jax.ShapeDtypeStruct((n_dev, padded, columns), jnp.bfloat16),
        in_specs=[vmem] * 13,
        out_specs=vmem,
        scratch_shapes=[
            pltpu.VMEM((n_dev, padded, tr_dev), jnp.bfloat16),
            pltpu.VMEM((n_dev, 1, tr_dev), jnp.int32),
            pltpu.VMEM((rec_l * padded, WIDE), jnp.float32),
            pltpu.VMEM((cmp_l * padded, WIDE), jnp.float32),
            pltpu.VMEM((padded, so_width), jnp.float32),
            pltpu.VMEM((rec_l * padded, WIDE), jnp.bfloat16),
            pltpu.VMEM((cmp_l * padded, WIDE), jnp.bfloat16),
            pltpu.VMEM((2 * padded, so_width), jnp.bfloat16),
            pltpu.VMEM((rec_l * padded, WIDE), jnp.float32),
            pltpu.VMEM((cmp_l * padded, WIDE), jnp.float32),
            pltpu.VMEM((n_dev * padded, columns), jnp.float32),
            pltpu.VMEM((n_dev, padded, tr_dev), jnp.bfloat16),
            pltpu.VMEM((1, tr_dev), jnp.int32),
            pltpu.VMEM((padded, tr_dev), jnp.float32),
            pltpu.VMEM((2 * rows, samples), jnp.bfloat16),
            pltpu.SemaphoreType.DMA((n_dev,)),
            pltpu.SemaphoreType.DMA((n_dev,)),
            pltpu.SemaphoreType.DMA((n_dev,)),
            pltpu.SemaphoreType.DMA((n_dev,)),
            pltpu.SemaphoreType.DMA((2,)),
        ],
        compiler_params=pltpu.CompilerParams(
            vmem_limit_bytes=VMEM_BYTES, collective_id=0, has_side_effects=True
        ),
        name="sweeps",
    )(traces, *ids, *tables, *owners)


def shards(traces, offset_bin, rec_id, cmp_id, rec_owner, rec_slot, cmp_owner, cmp_slot):
    shot_dev, tr_off, samples = traces.shape
    n_shot = lax.axis_size("shot")
    n_off = lax.axis_size("off")
    n_dev = n_shot * n_off
    tr_dev = shot_dev * tr_off
    rec_dev = rec_owner.shape[0] // n_shot
    cmp_dev = cmp_owner.shape[0] // n_shot
    rec_rows = rec_dev // n_off
    cmp_rows = cmp_dev // n_off
    held = up(NF, n_dev) // n_dev
    padded = up(held + 4, 8)
    columns = up(rec_rows + cmp_rows + shot_dev + OFFB_DEV, LANES)
    terms = run_sweeps(
        traces.reshape(tr_dev, samples),
        (offset_bin, rec_id, cmp_id),
        (rec_owner, rec_slot, cmp_owner, cmp_slot),
        (n_shot, n_off, shot_dev, held, rec_dev, cmp_dev),
        padded,
        columns,
    )
    base = rec_rows + cmp_rows
    splits = (rec_rows, base, base + OFFB_DEV, base + OFFB_DEV + shot_dev)
    return return_terms(terms, n_off, splits)


def solution(mesh):
    return jax.shard_map(
        shards,
        mesh=mesh,
        in_specs=(
            P("shot", "off", None),
            P("shot", "off"),
            P("shot", "off"),
            P("shot", "off"),
            P(),
            P(),
            P(),
            P(),
        ),
        out_specs=(
            P("shot", None),
            P("off", None),
            P(("shot", "off"), None),
            P(("shot", "off"), None),
        ),
        check_vma=False,
    )
```
